32 devices in a mesh: row: 8 (over y, x, core), col: 4 (over z).
Axes of the slice: x: 2, y: 2, z: 4, core: 2. Of those that a mesh axis runs over, the one named last changes fastest.
Arguments:
- amplitudes: bfloat16 [100, 100, 768], P(None, None, 'col'), may hold values from -6 to 6
- integrals: bfloat16 [768, 65536], P('col', 'row'), may hold values from -0.15625 to 0.15625
- blocks: int32 [8, 2], replicated, may hold values from 0 to 49, as said below
Outputs:
- residual: bfloat16 [32, 65536], P('col', 'row')
The draws below stay inside these ranges and needn't reach their ends.
Inputs may be any that keep to these rules, and one draw needn't show every extreme that they name: `blocks`: each row is a block pair (I, J) with I <= J, all rows distinct; the pair (0, 49) is always among them.
All inputs are finite; a program needn't handle non-finite values.
Results may differ from the reference program's by a relative error of at most 0.001.
Values may be sent and summed in bfloat16 or wider, within the bound.
A program may use at most 128 MiB of HBM per device.

```python
import jax
import jax.numpy as jnp
import numpy as np
from jax import lax

OCC = 100
OB = 2
NBO = 50
K = 768
AW = 256
NBLK = 8


def draw_blocks(key, part):
    pair_table = np.array([[upper, lower] for upper in range(NBO) for lower in range(upper, NBO)], dtype=np.int32)
    corner = NBO - 1
    count_all = pair_table.shape[0]
    ordering = np.concatenate([np.array([corner]), np.arange(corner), np.arange(corner + 1, count_all)])
    pair_table = jnp.asarray(pair_table[ordering])
    remaining = jax.random.permutation(jax.random.fold_in(key, 11), count_all - 1)[:NBLK - 1] + 1
    chosen = jnp.concatenate([jnp.zeros((1,), jnp.int32), remaining.astype(jnp.int32)])
    chosen = jax.random.permutation(jax.random.fold_in(key, 12), chosen)
    return pair_table[chosen].astype(jnp.int32)


def levels(rng, shape, pieces, least, high):
    def one(dim, shards_of):
        steps = jax.random.uniform(jax.random.fold_in(jax.random.fold_in(rng, 6), dim), (shards_of,), jnp.float32, least / len(pieces), high / len(pieces))
        return jnp.repeat(jnp.exp(steps), shape[dim] // shards_of).reshape((-1,) + (1,) * (len(shape) - dim - 1))

    level = one(*pieces[0])
    for cut in pieces[1:]:
        level = level * one(*cut)
    return level


def noise(own_key, dims, deviation, bound, split=(), kind=jnp.bfloat16):
    entries = jax.random.normal(own_key, dims, jnp.float32) * deviation
    if len(split) > 0:
        entries = levels(own_key, dims, split, -0.22, 0.18) * entries
    return jnp.clip(entries, min=-bound, max=bound).astype(kind)


def setup_inputs(seed: int = 0) -> dict:
    streams_of = jax.random.split(jax.random.key(seed), 4)
    amplitudes = noise(streams_of[0], (OCC, OCC, K), 1.0, 6.0, ((2, 4),))
    integrals = noise(streams_of[1], (K, AW * AW), (2 * K) ** -0.5, 0.15625, ((0, 4), (1, 8)))
    blocks = draw_blocks(jax.random.fold_in(streams_of[3], 71), 0)
    return dict(amplitudes=amplitudes, integrals=integrals, blocks=blocks)


def pick_rows(amplitudes, blocks):
    panel_width = amplitudes.shape[2]

    def one_block(pair_index):
        first_row = pair_index[0] * OB
        second_row = pair_index[1] * OB
        anchor = jnp.zeros((), jnp.int32)
        direct_rows = lax.dynamic_slice(amplitudes, (first_row, second_row, anchor), (OB, OB, panel_width))
        swapped_rows = lax.dynamic_slice(amplitudes, (second_row, first_row, anchor), (OB, OB, panel_width))
        return direct_rows.reshape(OB * OB, panel_width), jnp.swapaxes(swapped_rows, 0, 1).reshape(OB * OB, panel_width)

    direct_rows, swapped_rows = jax.vmap(one_block)(blocks)
    return direct_rows.reshape(-1, panel_width), swapped_rows.reshape(-1, panel_width)


def reference(amplitudes, integrals, blocks):
    forward, mirrored = pick_rows(amplitudes, blocks)
    depth = integrals.shape[0]
    flipped = jnp.swapaxes(integrals.reshape(depth, AW, AW), 1, 2).reshape(depth, AW * AW)
    total = jnp.dot(forward, integrals, preferred_element_type=jnp.float32) + jnp.dot(mirrored, flipped, preferred_element_type=jnp.float32)
    return total.astype(jnp.bfloat16)
```

```python
import functools
import math

import jax
import jax.numpy as jnp
from jax import lax
from jax.experimental import pallas as pl
from jax.experimental.pallas import tpu as pltpu
from jax.sharding import PartitionSpec as P

OB = 2
LANES = 128
ROWS = 8


def ladder_kernel(
    n_row, n_col, a_dev,
    blocks, amp_hbm, int_hbm, out_ref,
    amp, ints, lhs, prod, turned, inbox, from_left, from_right,
    amp_sem, int_sem, x_send, x_recv, r_send, r_recv, l_send, l_recv,
):
    row = lax.axis_index("row")
    col = lax.axis_index("col")
    pairs = lhs.shape[0] // 2
    width = a_dev * n_row
    tiles = width // LANES
    per_tile = LANES // a_dev
    share = pairs // n_col
    groups = share // per_tile
    occ = amp.shape[2]
    n_parts = int_sem.shape[0]
    part = ints.shape[1] // n_parts

    barrier = pltpu.get_barrier_semaphore()

    def greet(p, carry):
        pl.semaphore_signal(barrier, inc=1, device_id={"row": lax.rem(row + p, n_row)})
        return carry

    lax.fori_loop(1, n_row, greet, 0)

    @pl.when(col > 0)
    def _():
        pl.semaphore_signal(barrier, inc=1, device_id={"col": col - 1})

    @pl.when(col < n_col - 1)
    def _():
        pl.semaphore_signal(barrier, inc=1, device_id={"col": col + 1})

    amp_copy = pltpu.make_async_copy(amp_hbm, amp, amp_sem)
    amp_copy.start()
    int_copies = []
    for i in range(n_parts):
        cut = pl.ds(i * part, part)
        copy = pltpu.make_async_copy(int_hbm.at[:, cut], ints.at[:, cut], int_sem.at[i])
        copy.start()
        int_copies.append(copy)

    amp_copy.wait()
    spot_row = lax.broadcasted_iota(jnp.int32, (ROWS, occ), 0)
    spot_col = lax.broadcasted_iota(jnp.int32, (ROWS, occ), 1)

    def take(spots, plane):
        hit = jnp.zeros((ROWS, occ), jnp.bool_)
        for at, column in spots:
            hit = hit | ((spot_row == at) & (spot_col == column))
        chosen = jnp.where(hit, 1.0, 0.0).astype(amp.dtype)
        return lax.dot_general(
            chosen, amp[plane], (((1,), (1,)), ((), ())), preferred_element_type=jnp.float32
        )

    per_rows = ROWS // (OB * OB)
    for tile in range(pairs // ROWS):
        direct = jnp.zeros((ROWS, lhs.shape[1]), jnp.float32)
        swapped = direct
        for k in range(per_rows):
            upper = blocks[0, tile * per_rows + k] * OB
            lower = blocks[1, tile * per_rows + k] * OB
            base = k * OB * OB
            for m in range(OB):
                direct += take([(base + m * OB + v, lower + v) for v in range(OB)], upper + m)
                swapped += take([(base + u * OB + m, upper + u) for u in range(OB)], lower + m)
        lhs[tile * ROWS:(tile + 1) * ROWS, :] = direct
        lhs[pairs + tile * ROWS:pairs + (tile + 1) * ROWS, :] = swapped
    rows = lhs[...].astype(jnp.bfloat16)

    for i in range(n_parts):
        int_copies[i].wait()

        def one(step, carry, i=i):
            a = i * (part // width) + step
            panel = ints[:, pl.ds(pl.multiple_of(a * width, width), width)]
            got = jnp.dot(rows, panel, preferred_element_type=jnp.float32)
            for t in range(tiles):
                prod[t, pl.ds(a, 2 * pairs, stride=a_dev), :] = got[:, t * LANES:(t + 1) * LANES]
            return carry

        lax.fori_loop(0, part // width, one, 0, unroll=2)

    n_near = jnp.where(col > 0, 1, 0) + jnp.where(col < n_col - 1, 1, 0)
    pl.semaphore_wait(barrier, n_row - 1 + n_near)

    def order(s):
        return jnp.where(col < n_col // 2, n_col - 1 - s, s)

    def x_copy(d, p):
        peer = lax.rem(row + p, n_row)
        return pltpu.make_async_remote_copy(
            src_ref=turned.at[pl.ds(d * groups, groups), pl.ds(pl.multiple_of(peer * a_dev, a_dev), a_dev), :],
            dst_ref=inbox.at[d, row],
            send_sem=x_send.at[d, p],
            recv_sem=x_recv.at[d, p],
            device_id={"row": peer},
        )

    chunk = share * a_dev

    def mine(d, t, start=0, size=chunk):
        return prod.at[t, pl.ds(pl.multiple_of(d * chunk + start, a_dev), size)]

    def right_copy(d, t):
        return pltpu.make_async_remote_copy(
            src_ref=mine(d, t), dst_ref=from_left.at[d, t],
            send_sem=r_send.at[d, t], recv_sem=r_recv.at[d, t],
            device_id={"col": col + 1},
        )

    def left_copy(d, t):
        return pltpu.make_async_remote_copy(
            src_ref=mine(d, t), dst_ref=from_right.at[d, t],
            send_sem=l_send.at[d, t], recv_sem=l_recv.at[d, t],
            device_id={"col": col - 1},
        )

    def turn(s, carry):
        d = order(s)
        for g in range(groups):
            start = (pairs + d * share + g * per_tile) * a_dev
            for t in range(tiles):
                block = prod[t, pl.ds(pl.multiple_of(start, LANES), LANES), :]
                turned[d * groups + g, t * LANES:(t + 1) * LANES, :] = block.T

        def post(p, inner):
            x_copy(d, p).start()
            return inner

        lax.fori_loop(1, n_row, post, 0)
        return carry

    lax.fori_loop(0, n_col, turn, 0)

    piece = lax.broadcasted_iota(jnp.int32, (a_dev, LANES), 1) // a_dev

    def combine(s, carry):
        d = order(s)
        for g in range(groups):
            inbox[d, row, g] = turned[d * groups + g, pl.ds(pl.multiple_of(row * a_dev, a_dev), a_dev), :]
        for t in range(tiles):
            for j in range(per_tile):
                source = t * per_tile + j

                @pl.when(source != row)
                def _(source=source):
                    x_copy(d, lax.rem(row - source + n_row, n_row)).wait_recv()

            for g in range(groups):
                parts = [inbox[d, t * per_tile + j, g] for j in range(per_tile)]
                for q in range(per_tile):
                    merged = parts[q] if q == 0 else pltpu.roll(parts[0], (-q * a_dev) % LANES, 1)
                    for j in range(1, per_tile):
                        shift = ((j - q) * a_dev) % LANES
                        moved = pltpu.roll(parts[j], shift, 1) if shift else parts[j]
                        merged = jnp.where(piece == j, moved, merged)
                    here = mine(d, t, (g * per_tile + q) * a_dev, a_dev)
                    here[...] = here[...] + merged

            @pl.when(d > col)
            def _():
                @pl.when(col > 0)
                def _():
                    right_copy(d, t).wait_recv()
                    mine(d, t)[...] = mine(d, t)[...] + from_left[d, t]

                right_copy(d, t).start()

            @pl.when(d < col)
            def _():
                @pl.when(col < n_col - 1)
                def _():
                    left_copy(d, t).wait_recv()
                    mine(d, t)[...] = mine(d, t)[...] + from_right[d, t]

                left_copy(d, t).start()

        return carry

    lax.fori_loop(0, n_col, combine, 0)

    for t in range(tiles):
        @pl.when(col > 0)
        def _(t=t):
            right_copy(col, t).wait_recv()
            mine(col, t)[...] = mine(col, t)[...] + from_left[col, t]

        @pl.when(col < n_col - 1)
        def _(t=t):
            left_copy(col, t).wait_recv()
            mine(col, t)[...] = mine(col, t)[...] + from_right[col, t]

        for a in range(a_dev):
            value = prod[t, pl.ds(col * chunk + a, share, stride=a_dev), :]
            at = a * width + t * LANES
            out_ref[:, at:at + LANES] = value.astype(out_ref.dtype)

    def finish(d, carry):
        def sent(p, inner):
            x_copy(d, p).wait_send()
            return inner

        lax.fori_loop(1, n_row, sent, 0)
        for t in range(tiles):
            @pl.when(d > col)
            def _(t=t):
                right_copy(d, t).wait_send()

            @pl.when(d < col)
            def _(t=t):
                left_copy(d, t).wait_send()

        return carry

    lax.fori_loop(0, n_col, finish, 0)


def on_device(n_row, n_col, amplitudes, integrals, blocks):
    amplitudes = jnp.swapaxes(amplitudes, 1, 2)
    blocks = blocks.T
    depth, local = integrals.shape
    width = math.isqrt(local * n_row)
    a_dev = width // n_row
    pairs = blocks.shape[1] * OB * OB
    tiles = width // LANES
    share = pairs // n_col
    groups = share * a_dev // LANES
    n_parts = 4
    f32 = jnp.float32
    dma = pltpu.SemaphoreType.DMA
    return pl.pallas_call(
        functools.partial(ladder_kernel, n_row, n_col, a_dev),
        out_shape=jax.ShapeDtypeStruct((share, local), jnp.bfloat16),
        in_specs=[
            pl.BlockSpec(memory_space=pltpu.SMEM),
            pl.BlockSpec(memory_space=pl.ANY),
            pl.BlockSpec(memory_space=pl.ANY),
        ],
        out_specs=pl.BlockSpec(memory_space=pltpu.VMEM),
        scratch_shapes=[
            pltpu.VMEM(amplitudes.shape, amplitudes.dtype),
            pltpu.VMEM(integrals.shape, integrals.dtype),
            pltpu.VMEM((2 * pairs, depth), f32),
            pltpu.VMEM((tiles, 2 * pairs * a_dev, LANES), f32),
            pltpu.VMEM((n_col * groups, width, LANES), f32),
            pltpu.VMEM((n_col, n_row, groups, a_dev, LANES), f32),
            pltpu.VMEM((n_col, tiles, share * a_dev, LANES), f32),
            pltpu.VMEM((n_col, tiles, share * a_dev, LANES), f32),
            dma(()),
            dma((n_parts,)),
            dma((n_col, n_row)),
            dma((n_col, n_row)),
            dma((n_col, tiles)),
            dma((n_col, tiles)),
            dma((n_col, tiles)),
            dma((n_col, tiles)),
        ],
        compiler_params=pltpu.CompilerParams(
            collective_id=0, has_side_effects=True, vmem_limit_bytes=67043328
        ),
    )(blocks, amplitudes, integrals)


def solution(mesh):
    return jax.shard_map(
        functools.partial(on_device, mesh.shape["row"], mesh.shape["col"]),
        mesh=mesh,
        in_specs=(P(None, None, "col"), P("col", "row"), P()),
        out_specs=P("col", "row"),
        check_vma=False,
    )
```

```python
import functools
import math

import jax
import jax.numpy as jnp
from jax import lax
from jax.experimental import pallas as pl
from jax.experimental.pallas import tpu as pltpu
from jax.sharding import PartitionSpec as P

OB = 2
LANES = 128
CODES = 256.0
SCALE = 256.0 * 127.0
TINY = 1e-30
ROWS = 8


def ladder_kernel(
    n_row, n_col, a_dev,
    blocks, amp_hbm, int_hbm, out_ref,
    amp, ints, lhs, prod, turned, inbox,
    main_out, rest_out, main_left, rest_left, main_right, rest_right,
    amp_sem, int_sem, x_send, x_recv, r_send, r_recv, l_send, l_recv,
):
    row = lax.axis_index("row")
    col = lax.axis_index("col")
    pairs = lhs.shape[0] // 2
    width = a_dev * n_row
    tiles = width // LANES
    per_tile = LANES // a_dev
    share = pairs // n_col
    groups = share // per_tile
    occ = amp.shape[2]
    n_parts = int_sem.shape[0]
    part = ints.shape[1] // n_parts

    barrier = pltpu.get_barrier_semaphore()

    def greet(p, carry):
        pl.semaphore_signal(barrier, inc=1, device_id={"row": lax.rem(row + p, n_row)})
        return carry

    lax.fori_loop(1, n_row, greet, 0)

    @pl.when(col > 0)
    def _():
        pl.semaphore_signal(barrier, inc=1, device_id={"col": col - 1})

    @pl.when(col < n_col - 1)
    def _():
        pl.semaphore_signal(barrier, inc=1, device_id={"col": col + 1})

    amp_copy = pltpu.make_async_copy(amp_hbm, amp, amp_sem)
    amp_copy.start()
    int_copies = []
    for i in range(n_parts):
        cut = pl.ds(i * part, part)
        copy = pltpu.make_async_copy(int_hbm.at[:, cut], ints.at[:, cut], int_sem.at[i])
        copy.start()
        int_copies.append(copy)

    amp_copy.wait()
    spot_row = lax.broadcasted_iota(jnp.int32, (ROWS, occ), 0)
    spot_col = lax.broadcasted_iota(jnp.int32, (ROWS, occ), 1)

    def take(spots, plane):
        hit = jnp.zeros((ROWS, occ), jnp.bool_)
        for at, column in spots:
            hit = hit | ((spot_row == at) & (spot_col == column))
        chosen = jnp.where(hit, 1.0, 0.0).astype(amp.dtype)
        return lax.dot_general(
            chosen, amp[plane], (((1,), (1,)), ((), ())), preferred_element_type=jnp.float32
        )

    per_rows = ROWS // (OB * OB)
    for tile in range(pairs // ROWS):
        direct = jnp.zeros((ROWS, lhs.shape[1]), jnp.float32)
        swapped = direct
        for k in range(per_rows):
            upper = blocks[0, tile * per_rows + k] * OB
            lower = blocks[1, tile * per_rows + k] * OB
            base = k * OB * OB
            for m in range(OB):
                direct += take([(base + m * OB + v, lower + v) for v in range(OB)], upper + m)
                swapped += take([(base + u * OB + m, upper + u) for u in range(OB)], lower + m)
        lhs[tile * ROWS:(tile + 1) * ROWS, :] = direct
        lhs[pairs + tile * ROWS:pairs + (tile + 1) * ROWS, :] = swapped
    rows = lhs[...].astype(jnp.bfloat16)

    for i in range(n_parts):
        int_copies[i].wait()

        def one(step, carry, i=i):
            a = i * (part // width) + step
            panel = ints[:, pl.ds(pl.multiple_of(a * width, width), width)]
            got = jnp.dot(rows, panel, preferred_element_type=jnp.float32)
            for t in range(tiles):
                prod[t, pl.ds(a, 2 * pairs, stride=a_dev), :] = got[:, t * LANES:(t + 1) * LANES]
            return carry

        lax.fori_loop(0, part // width, one, 0, unroll=8)

    n_near = jnp.where(col > 0, 1, 0) + jnp.where(col < n_col - 1, 1, 0)
    pl.semaphore_wait(barrier, n_row - 1 + n_near)

    def order(s):
        return jnp.where(col < n_col // 2, n_col - 1 - s, s)

    def x_copy(d, g, p):
        peer = lax.rem(row + p, n_row)
        return pltpu.make_async_remote_copy(
            src_ref=turned.at[d * groups + g, pl.ds(pl.multiple_of(peer * a_dev, a_dev), a_dev), :],
            dst_ref=inbox.at[d, g, row],
            send_sem=x_send.at[d, g, p],
            recv_sem=x_recv.at[d, g, p],
            device_id={"row": peer},
        )

    def z_copies(d, g, right):
        send, recv = (r_send, r_recv) if right else (l_send, l_recv)
        main_in, rest_in = (main_left, rest_left) if right else (main_right, rest_right)
        to = col + 1 if right else col - 1
        return [
            pltpu.make_async_remote_copy(
                src_ref=src.at[d, g], dst_ref=dst.at[d, g],
                send_sem=send.at[d, g, i], recv_sem=recv.at[d, g, i],
                device_id={"col": to},
            )
            for i, (src, dst) in enumerate(((main_out, main_in), (rest_out, rest_in)))
        ]

    def held(d, g, t):
        start = pl.multiple_of(d * (share * a_dev) + g * LANES, LANES)
        return prod.at[t, pl.ds(start, LANES)]

    half = tiles // 2

    def add_from(d, g, right):
        for copy in z_copies(d, g, right):
            copy.wait_recv()
        main_in, rest_in = (main_left, rest_left) if right else (main_right, rest_right)
        for t in range(half):
            word = rest_in[d, g, t].astype(jnp.int32).astype(jnp.float32)
            high = jnp.round(word * (1.0 / CODES))
            for place, code in ((t, high), (t + half, word - high * CODES)):
                main = main_in[d, g, place].astype(jnp.float32)
                step = jnp.maximum(jnp.abs(main), TINY) * (1.0 / SCALE)
                here = held(d, g, place)
                here[...] = here[...] + (main + code * step)

    def send_on(d, g, right):
        for t in range(half):
            codes = []
            for place in (t, t + half):
                value = held(d, g, place)[...]
                main = value.astype(jnp.bfloat16)
                main_out[d, g, place] = main
                main = main.astype(jnp.float32)
                codes.append(jnp.round((value - main) * (SCALE / jnp.maximum(jnp.abs(main), TINY))))
            word = codes[0] * CODES + codes[1]
            rest_out[d, g, t] = word.astype(jnp.int32).astype(jnp.int16)
        for copy in z_copies(d, g, right):
            copy.start()

    def turn(s, carry):
        d = order(s)
        for g in range(groups):
            start = (pairs + d * share + g * per_tile) * a_dev
            for t in range(tiles):
                block = prod[t, pl.ds(pl.multiple_of(start, LANES), LANES), :]
                turned[d * groups + g, t * LANES:(t + 1) * LANES, :] = block.T

            def post(p, inner, g=g):
                x_copy(d, g, p).start()
                return inner

            lax.fori_loop(1, n_row, post, 0)
        return carry

    lax.fori_loop(0, n_col, turn, 0)

    piece = lax.broadcasted_iota(jnp.int32, (a_dev, LANES), 1) // a_dev

    def combine(s, carry):
        d = order(s)
        for g in range(groups):
            inbox[d, g, row] = turned[d * groups + g, pl.ds(pl.multiple_of(row * a_dev, a_dev), a_dev), :]

            def arrived(p, inner, g=g):
                x_copy(d, g, p).wait_recv()
                return inner

            lax.fori_loop(1, n_row, arrived, 0)
            for t in range(tiles):
                parts = [inbox[d, g, t * per_tile + j] for j in range(per_tile)]
                sums = []
                for q in range(per_tile):
                    merged = pltpu.roll(parts[0], (-q * a_dev) % LANES, 1) if q else parts[0]
                    for j in range(1, per_tile):
                        shift = ((j - q) * a_dev) % LANES
                        moved = pltpu.roll(parts[j], shift, 1) if shift else parts[j]
                        merged = jnp.where(piece == j, moved, merged)
                    sums.append(merged)
                here = held(d, g, t)
                here[...] = here[...] + jnp.concatenate(sums, axis=0)

            @pl.when(d > col)
            def _(g=g):
                @pl.when(col > 0)
                def _():
                    add_from(d, g, True)

                send_on(d, g, True)

            @pl.when(d < col)
            def _(g=g):
                @pl.when(col < n_col - 1)
                def _():
                    add_from(d, g, False)

                send_on(d, g, False)

        return carry

    lax.fori_loop(0, n_col, combine, 0)

    for g in range(groups):
        @pl.when(col > 0)
        def _(g=g):
            add_from(col, g, True)

        @pl.when(col < n_col - 1)
        def _(g=g):
            add_from(col, g, False)

    for t in range(tiles):
        for a in range(a_dev):
            value = prod[t, pl.ds(col * (share * a_dev) + a, share, stride=a_dev), :]
            at = a * width + t * LANES
            out_ref[:, at:at + LANES] = value.astype(out_ref.dtype)

    def finish(d, carry):
        for g in range(groups):
            def sent(p, inner, g=g):
                x_copy(d, g, p).wait_send()
                return inner

            lax.fori_loop(1, n_row, sent, 0)

            @pl.when(d > col)
            def _(g=g):
                for copy in z_copies(d, g, True):
                    copy.wait_send()

            @pl.when(d < col)
            def _(g=g):
                for copy in z_copies(d, g, False):
                    copy.wait_send()

        return carry

    lax.fori_loop(0, n_col, finish, 0)


def on_device(n_row, n_col, amplitudes, integrals, blocks):
    amplitudes = jnp.swapaxes(amplitudes, 1, 2)
    blocks = blocks.T
    depth, local = integrals.shape
    width = math.isqrt(local * n_row)
    a_dev = width // n_row
    pairs = blocks.shape[1] * OB * OB
    tiles = width // LANES
    share = pairs // n_col
    groups = share * a_dev // LANES
    n_parts = 4
    f32 = jnp.float32
    dma = pltpu.SemaphoreType.DMA
    coded = [
        pltpu.VMEM((n_col, groups, tiles, LANES, LANES), jnp.bfloat16),
        pltpu.VMEM((n_col, groups, tiles // 2, LANES, LANES), jnp.int16),
    ]
    return pl.pallas_call(
        functools.partial(ladder_kernel, n_row, n_col, a_dev),
        out_shape=jax.ShapeDtypeStruct((share, local), jnp.bfloat16),
        in_specs=[
            pl.BlockSpec(memory_space=pltpu.SMEM),
            pl.BlockSpec(memory_space=pl.ANY),
            pl.BlockSpec(memory_space=pl.ANY),
        ],
        out_specs=pl.BlockSpec(memory_space=pltpu.VMEM),
        scratch_shapes=[
            pltpu.VMEM(amplitudes.shape, amplitudes.dtype),
            pltpu.VMEM(integrals.shape, integrals.dtype),
            pltpu.VMEM((2 * pairs, depth), f32),
            pltpu.VMEM((tiles, 2 * pairs * a_dev, LANES), f32),
            pltpu.VMEM((n_col * groups, width, LANES), f32),
            pltpu.VMEM((n_col, groups, n_row, a_dev, LANES), f32),
            *coded, *coded, *coded,
            dma(()),
            dma((n_parts,)),
            dma((n_col, groups, n_row)),
            dma((n_col, groups, n_row)),
            dma((n_col, groups, 2)),
            dma((n_col, groups, 2)),
            dma((n_col, groups, 2)),
            dma((n_col, groups, 2)),
        ],
        compiler_params=pltpu.CompilerParams(
            collective_id=0, has_side_effects=True, vmem_limit_bytes=67043328
        ),
    )(blocks, amplitudes, integrals)


def solution(mesh):
    return jax.shard_map(
        functools.partial(on_device, mesh.shape["row"], mesh.shape["col"]),
        mesh=mesh,
        in_specs=(P(None, None, "col"), P("col", "row"), P()),
        out_specs=P("col", "row"),
        check_vma=False,
    )
```

```python
import functools
import math

import jax
import jax.numpy as jnp
from jax import lax
from jax.experimental import pallas as pl
from jax.experimental.pallas import tpu as pltpu
from jax.sharding import PartitionSpec as P

OB = 2
LANES = 128
CODES = 256.0
SCALE = 256.0 * 127.0
TINY = 1e-30
ROWS = 8


def ladder_kernel(
    n_row, n_col, a_dev,
    blocks, amp_hbm, int_hbm, out_ref,
    amp, ints, lhs, prod, turned, inbox,
    main_out, rest_out, main_left, rest_left, main_right, rest_right,
    amp_sem, int_sem, x_send, x_recv, r_send, r_recv, l_send, l_recv,
):
    row = lax.axis_index("row")
    col = lax.axis_index("col")
    pairs = lhs.shape[0] // 2
    width = a_dev * n_row
    tiles = width // LANES
    per_tile = LANES // a_dev
    share = pairs // n_col
    groups = share // per_tile
    occ = amp.shape[2]
    n_parts = int_sem.shape[0]
    part = ints.shape[1] // n_parts

    barrier = pltpu.get_barrier_semaphore()

    def greet(p, carry):
        pl.semaphore_signal(barrier, inc=1, device_id={"row": lax.rem(row + p, n_row)})
        return carry

    lax.fori_loop(1, n_row, greet, 0)

    @pl.when(col > 0)
    def _():
        pl.semaphore_signal(barrier, inc=1, device_id={"col": col - 1})

    @pl.when(col < n_col - 1)
    def _():
        pl.semaphore_signal(barrier, inc=1, device_id={"col": col + 1})

    amp_copy = pltpu.make_async_copy(amp_hbm, amp, amp_sem)
    amp_copy.start()
    int_copies = []
    for i in range(n_parts):
        cut = pl.ds(i * part, part)
        copy = pltpu.make_async_copy(int_hbm.at[:, cut], ints.at[:, cut], int_sem.at[i])
        copy.start()
        int_copies.append(copy)

    amp_copy.wait()
    spot_row = lax.broadcasted_iota(jnp.int32, (ROWS, occ), 0)
    spot_col = lax.broadcasted_iota(jnp.int32, (ROWS, occ), 1)

    def take(spots, plane):
        hit = jnp.zeros((ROWS, occ), jnp.bool_)
        for at, column in spots:
            hit = hit | ((spot_row == at) & (spot_col == column))
        chosen = jnp.where(hit, 1.0, 0.0).astype(amp.dtype)
        return lax.dot_general(
            chosen, amp[plane], (((1,), (1,)), ((), ())), preferred_element_type=jnp.float32
        )

    per_rows = ROWS // (OB * OB)
    for tile in range(pairs // ROWS):
        direct = jnp.zeros((ROWS, lhs.shape[1]), jnp.float32)
        swapped = direct
        for k in range(per_rows):
            upper = blocks[0, tile * per_rows + k] * OB
            lower = blocks[1, tile * per_rows + k] * OB
            base = k * OB * OB
            for m in range(OB):
                direct += take([(base + m * OB + v, lower + v) for v in range(OB)], upper + m)
                swapped += take([(base + u * OB + m, upper + u) for u in range(OB)], lower + m)
        lhs[tile * ROWS:(tile + 1) * ROWS, :] = direct
        lhs[pairs + tile * ROWS:pairs + (tile + 1) * ROWS, :] = swapped
    rows = lhs[...].astype(jnp.bfloat16)

    def multiply(i, first):
        block = rows[first:first + pairs]

        def one(step, carry):
            a = i * (part // width) + step
            panel = ints[:, pl.ds(pl.multiple_of(a * width, width), width)]
            got = jnp.dot(block, panel, preferred_element_type=jnp.float32)
            for t in range(tiles):
                prod[t, pl.ds(first * a_dev + a, pairs, stride=a_dev), :] = got[:, t * LANES:(t + 1) * LANES]
            return carry

        lax.fori_loop(0, part // width, one, 0, unroll=8)

    for i in range(n_parts):
        int_copies[i].wait()
        multiply(i, pairs)

    n_near = jnp.where(col > 0, 1, 0) + jnp.where(col < n_col - 1, 1, 0)
    pl.semaphore_wait(barrier, n_row - 1 + n_near)

    to_right = n_col - 1 - col
    near = jnp.minimum(col, to_right)
    lone = (jnp.maximum(col, to_right) - near) * groups
    outward = jnp.where(to_right >= col, 1, -1)

    def unit(k):
        rest = jnp.maximum(k - lone, 0)
        distance = near - rest // (2 * groups)
        within = rest % (2 * groups)
        side = jnp.where(within % 2 == 0, -outward, outward)
        is_lone = k < lone
        is_own = distance == 0
        shift = jnp.where(is_lone, outward * (near + (lone - 1 - k) // groups + 1), side * distance)
        g = jnp.where(is_lone, k % groups, jnp.where(is_own, within, within // 2))
        return col + shift, g

    def x_copy(d, g, p):
        peer = lax.rem(row + p, n_row)
        return pltpu.make_async_remote_copy(
            src_ref=turned.at[d * groups + g, pl.ds(pl.multiple_of(peer * a_dev, a_dev), a_dev), :],
            dst_ref=inbox.at[d, g, row],
            send_sem=x_send.at[d, g, p],
            recv_sem=x_recv.at[d, g, p],
            device_id={"row": peer},
        )

    def z_copies(d, g, right):
        send, recv = (r_send, r_recv) if right else (l_send, l_recv)
        main_in, rest_in = (main_left, rest_left) if right else (main_right, rest_right)
        to = col + 1 if right else col - 1
        return [
            pltpu.make_async_remote_copy(
                src_ref=src.at[d, g], dst_ref=dst.at[d, g],
                send_sem=send.at[d, g, i], recv_sem=recv.at[d, g, i],
                device_id={"col": to},
            )
            for i, (src, dst) in enumerate(((main_out, main_in), (rest_out, rest_in)))
        ]

    def held(d, g, t):
        start = pl.multiple_of(d * (share * a_dev) + g * LANES, LANES)
        return prod.at[t, pl.ds(start, LANES)]

    half = tiles // 2

    def add_from(d, g, right):
        for copy in z_copies(d, g, right):
            copy.wait_recv()
        main_in, rest_in = (main_left, rest_left) if right else (main_right, rest_right)
        for t in range(half):
            word = rest_in[d, g, t].astype(jnp.int32).astype(jnp.float32)
            high = jnp.round(word * (1.0 / CODES))
            for place, code in ((t, high), (t + half, word - high * CODES)):
                main = main_in[d, g, place].astype(jnp.float32)
                step = jnp.maximum(jnp.abs(main), TINY) * (1.0 / SCALE)
                here = held(d, g, place)
                here[...] = here[...] + (main + code * step)

    def send_on(d, g, right):
        for t in range(half):
            codes = []
            for place in (t, t + half):
                value = held(d, g, place)[...]
                main = value.astype(jnp.bfloat16)
                main_out[d, g, place] = main
                main = main.astype(jnp.float32)
                codes.append(jnp.round((value - main) * (SCALE / jnp.maximum(jnp.abs(main), TINY))))
            word = codes[0] * CODES + codes[1]
            rest_out[d, g, t] = word.astype(jnp.int32).astype(jnp.int16)
        for copy in z_copies(d, g, right):
            copy.start()

    def turn(k, carry):
        d, g = unit(k)
        start = (pairs + d * share + g * per_tile) * a_dev
        for t in range(tiles):
            block = prod[t, pl.ds(pl.multiple_of(start, LANES), LANES), :]
            turned[d * groups + g, t * LANES:(t + 1) * LANES, :] = block.T

        def post(p, inner):
            x_copy(d, g, p).start()
            return inner

        lax.fori_loop(1, n_row, post, 0)
        return carry

    lax.fori_loop(0, n_col * groups, turn, 0)

    for i in range(n_parts):
        multiply(i, 0)

    piece = lax.broadcasted_iota(jnp.int32, (a_dev, LANES), 1) // a_dev

    def combine(k, carry):
        d, g = unit(k)
        inbox[d, g, row] = turned[d * groups + g, pl.ds(pl.multiple_of(row * a_dev, a_dev), a_dev), :]

        def arrived(p, inner):
            x_copy(d, g, p).wait_recv()
            return inner

        lax.fori_loop(1, n_row, arrived, 0)
        for t in range(tiles):
            parts = [inbox[d, g, t * per_tile + j] for j in range(per_tile)]
            sums = []
            for q in range(per_tile):
                merged = pltpu.roll(parts[0], (-q * a_dev) % LANES, 1) if q else parts[0]
                for j in range(1, per_tile):
                    shift = ((j - q) * a_dev) % LANES
                    moved = pltpu.roll(parts[j], shift, 1) if shift else parts[j]
                    merged = jnp.where(piece == j, moved, merged)
                sums.append(merged)
            here = held(d, g, t)
            here[...] = here[...] + jnp.concatenate(sums, axis=0)

        @pl.when(d > col)
        def _():
            @pl.when(col > 0)
            def _():
                add_from(d, g, True)

            send_on(d, g, True)

        @pl.when(d < col)
        def _():
            @pl.when(col < n_col - 1)
            def _():
                add_from(d, g, False)

            send_on(d, g, False)

        return carry

    lax.fori_loop(0, n_col * groups, combine, 0)

    for g in range(groups):
        @pl.when(col > 0)
        def _(g=g):
            add_from(col, g, True)

        @pl.when(col < n_col - 1)
        def _(g=g):
            add_from(col, g, False)

    for t in range(tiles):
        for a in range(a_dev):
            value = prod[t, pl.ds(col * (share * a_dev) + a, share, stride=a_dev), :]
            at = a * width + t * LANES
            out_ref[:, at:at + LANES] = value.astype(out_ref.dtype)

    def finish(d, carry):
        for g in range(groups):
            def sent(p, inner, g=g):
                x_copy(d, g, p).wait_send()
                return inner

            lax.fori_loop(1, n_row, sent, 0)

            @pl.when(d > col)
            def _(g=g):
                for copy in z_copies(d, g, True):
                    copy.wait_send()

            @pl.when(d < col)
            def _(g=g):
                for copy in z_copies(d, g, False):
                    copy.wait_send()

        return carry

    lax.fori_loop(0, n_col, finish, 0)


def on_device(n_row, n_col, amplitudes, integrals, blocks):
    amplitudes = jnp.swapaxes(amplitudes, 1, 2)
    blocks = blocks.T
    depth, local = integrals.shape
    width = math.isqrt(local * n_row)
    a_dev = width // n_row
    pairs = blocks.shape[1] * OB * OB
    tiles = width // LANES
    share = pairs // n_col
    groups = share * a_dev // LANES
    n_parts = 4
    f32 = jnp.float32
    dma = pltpu.SemaphoreType.DMA
    coded = [
        pltpu.VMEM((n_col, groups, tiles, LANES, LANES), jnp.bfloat16),
        pltpu.VMEM((n_col, groups, tiles // 2, LANES, LANES), jnp.int16),
    ]
    return pl.pallas_call(
        functools.partial(ladder_kernel, n_row, n_col, a_dev),
        out_shape=jax.ShapeDtypeStruct((share, local), jnp.bfloat16),
        in_specs=[
            pl.BlockSpec(memory_space=pltpu.SMEM),
            pl.BlockSpec(memory_space=pl.ANY),
            pl.BlockSpec(memory_space=pl.ANY),
        ],
        out_specs=pl.BlockSpec(memory_space=pltpu.VMEM),
        scratch_shapes=[
            pltpu.VMEM(amplitudes.shape, amplitudes.dtype),
            pltpu.VMEM(integrals.shape, integrals.dtype),
            pltpu.VMEM((2 * pairs, depth), f32),
            pltpu.VMEM((tiles, 2 * pairs * a_dev, LANES), f32),
            pltpu.VMEM((n_col * groups, width, LANES), f32),
            pltpu.VMEM((n_col, groups, n_row, a_dev, LANES), f32),
            *coded, *coded, *coded,
            dma(()),
            dma((n_parts,)),
            dma((n_col, groups, n_row)),
            dma((n_col, groups, n_row)),
            dma((n_col, groups, 2)),
            dma((n_col, groups, 2)),
            dma((n_col, groups, 2)),
            dma((n_col, groups, 2)),
        ],
        compiler_params=pltpu.CompilerParams(
            collective_id=0, has_side_effects=True, vmem_limit_bytes=67043328
        ),
    )(blocks, amplitudes, integrals)


def solution(mesh):
    return jax.shard_map(
        functools.partial(on_device, mesh.shape["row"], mesh.shape["col"]),
        mesh=mesh,
        in_specs=(P(None, None, "col"), P("col", "row"), P()),
        out_specs=P("col", "row"),
        check_vma=False,
    )
```

```python
import functools
import math

import jax
import jax.numpy as jnp
from jax import lax
from jax.experimental import pallas as pl
from jax.experimental.pallas import tpu as pltpu
from jax.sharding import PartitionSpec as P

OB = 2
LANES = 128
CODES = 256.0
SCALE = 256.0 * 127.0
TINY = 1e-30
ROWS = 8


def ladder_kernel(
    n_row, n_col, a_dev,
    blocks, amp_hbm, int_hbm, out_ref,
    amp, ints, lhs, prod, turned, inbox,
    main_out, rest_out, main_left, rest_left, main_right, rest_right,
    amp_sem, int_sem, x_send, x_recv, r_send, r_recv, l_send, l_recv,
):
    row = lax.axis_index("row")
    col = lax.axis_index("col")
    pairs = lhs.shape[0] // 2
    width = a_dev * n_row
    tiles = width // LANES
    per_tile = LANES // a_dev
    share = pairs // n_col
    groups = share // per_tile
    occ = amp.shape[2]
    n_parts = int_sem.shape[0]
    part = ints.shape[1] // n_parts

    barrier = pltpu.get_barrier_semaphore()

    def greet(p, carry):
        pl.semaphore_signal(barrier, inc=1, device_id={"row": lax.rem(row + p, n_row)})
        return carry

    lax.fori_loop(1, n_row, greet, 0)

    @pl.when(col > 0)
    def _():
        pl.semaphore_signal(barrier, inc=1, device_id={"col": col - 1})

    @pl.when(col < n_col - 1)
    def _():
        pl.semaphore_signal(barrier, inc=1, device_id={"col": col + 1})

    amp_copy = pltpu.make_async_copy(amp_hbm, amp, amp_sem)
    amp_copy.start()
    int_copies = []
    for i in range(n_parts):
        cut = pl.ds(i * part, part)
        copy = pltpu.make_async_copy(int_hbm.at[:, cut], ints.at[:, cut], int_sem.at[i])
        if i < n_parts // 2:
            copy.start()
        int_copies.append(copy)

    amp_copy.wait()
    for copy in int_copies[n_parts // 2:]:
        copy.start()
    spot_row = lax.broadcasted_iota(jnp.int32, (ROWS, occ), 0)
    spot_col = lax.broadcasted_iota(jnp.int32, (ROWS, occ), 1)

    def take(spots, plane):
        hit = jnp.zeros((ROWS, occ), jnp.bool_)
        for at, column in spots:
            hit = hit | ((spot_row == at) & (spot_col == column))
        chosen = jnp.where(hit, 1.0, 0.0).astype(amp.dtype)
        return lax.dot_general(
            chosen, amp[plane], (((1,), (1,)), ((), ())), preferred_element_type=jnp.float32
        )

    per_rows = ROWS // (OB * OB)

    def gather(mirrored):
        for tile in range(pairs // ROWS):
            found = jnp.zeros((ROWS, lhs.shape[1]), jnp.float32)
            for k in range(per_rows):
                upper = blocks[0, tile * per_rows + k] * OB
                lower = blocks[1, tile * per_rows + k] * OB
                base = k * OB * OB
                for m in range(OB):
                    if mirrored:
                        found += take([(base + u * OB + m, upper + u) for u in range(OB)], lower + m)
                    else:
                        found += take([(base + m * OB + v, lower + v) for v in range(OB)], upper + m)
            at = (pairs if mirrored else 0) + tile * ROWS
            lhs[at:at + ROWS, :] = found

    gather(True)

    def multiply(i, first):
        block = lhs[first:first + pairs, :].astype(jnp.bfloat16)

        def one(step, carry):
            a = i * (part // width) + step
            panel = ints[:, pl.ds(pl.multiple_of(a * width, width), width)]
            got = jnp.dot(block, panel, preferred_element_type=jnp.float32)
            for t in range(tiles):
                prod[t, pl.ds(first * a_dev + a, pairs, stride=a_dev), :] = got[:, t * LANES:(t + 1) * LANES]
            return carry

        lax.fori_loop(0, part // width, one, 0, unroll=8)

    for i in range(n_parts):
        int_copies[i].wait()
        multiply(i, pairs)

    n_near = jnp.where(col > 0, 1, 0) + jnp.where(col < n_col - 1, 1, 0)
    pl.semaphore_wait(barrier, n_row - 1 + n_near)

    to_right = n_col - 1 - col
    near = jnp.minimum(col, to_right)
    lone = (jnp.maximum(col, to_right) - near) * groups
    outward = jnp.where(to_right >= col, 1, -1)

    def unit(k):
        rest = jnp.maximum(k - lone, 0)
        distance = near - rest // (2 * groups)
        within = rest % (2 * groups)
        side = jnp.where(within % 2 == 0, -outward, outward)
        is_lone = k < lone
        is_own = distance == 0
        shift = jnp.where(is_lone, outward * (near + (lone - 1 - k) // groups + 1), side * distance)
        g = jnp.where(is_lone, k % groups, jnp.where(is_own, within, within // 2))
        return col + shift, g

    def x_copy(d, g, p):
        peer = lax.rem(row + p, n_row)
        return pltpu.make_async_remote_copy(
            src_ref=turned.at[d * groups + g, pl.ds(pl.multiple_of(peer * a_dev, a_dev), a_dev), :],
            dst_ref=inbox.at[d, g, row],
            send_sem=x_send.at[d, g, p],
            recv_sem=x_recv.at[d, g, p],
            device_id={"row": peer},
        )

    def z_copies(d, g, right):
        send, recv = (r_send, r_recv) if right else (l_send, l_recv)
        main_in, rest_in = (main_left, rest_left) if right else (main_right, rest_right)
        to = col + 1 if right else col - 1
        return [
            pltpu.make_async_remote_copy(
                src_ref=src.at[d, g], dst_ref=dst.at[d, g],
                send_sem=send.at[d, g, i], recv_sem=recv.at[d, g, i],
                device_id={"col": to},
            )
            for i, (src, dst) in enumerate(((main_out, main_in), (rest_out, rest_in)))
        ]

    def held(d, g, t):
        start = pl.multiple_of(d * (share * a_dev) + g * LANES, LANES)
        return prod.at[t, pl.ds(start, LANES)]

    half = tiles // 2

    def add_from(d, g, right):
        for copy in z_copies(d, g, right):
            copy.wait_recv()
        main_in, rest_in = (main_left, rest_left) if right else (main_right, rest_right)
        for t in range(half):
            word = rest_in[d, g, t].astype(jnp.int32).astype(jnp.float32)
            high = jnp.round(word * (1.0 / CODES))
            for place, code in ((t, high), (t + half, word - high * CODES)):
                main = main_in[d, g, place].astype(jnp.float32)
                step = jnp.maximum(jnp.abs(main), TINY) * (1.0 / SCALE)
                here = held(d, g, place)
                here[...] = here[...] + (main + code * step)

    def send_on(d, g, right):
        for t in range(half):
            codes = []
            for place in (t, t + half):
                value = held(d, g, place)[...]
                main = value.astype(jnp.bfloat16)
                main_out[d, g, place] = main
                main = main.astype(jnp.float32)
                codes.append(jnp.round((value - main) * (SCALE / jnp.maximum(jnp.abs(main), TINY))))
            word = codes[0] * CODES + codes[1]
            rest_out[d, g, t] = word.astype(jnp.int32).astype(jnp.int16)
        for copy in z_copies(d, g, right):
            copy.start()

    def turn(k, carry):
        d, g = unit(k)
        start = (pairs + d * share + g * per_tile) * a_dev
        for t in range(tiles):
            block = prod[t, pl.ds(pl.multiple_of(start, LANES), LANES), :]
            turned[d * groups + g, t * LANES:(t + 1) * LANES, :] = block.T

        def post(p, inner):
            x_copy(d, g, p).start()
            return inner

        lax.fori_loop(1, n_row, post, 0)
        return carry

    lax.fori_loop(0, n_col * groups, turn, 0)

    gather(False)
    for i in range(n_parts):
        multiply(i, 0)

    piece = lax.broadcasted_iota(jnp.int32, (a_dev, LANES), 1) // a_dev

    def combine(k, carry):
        d, g = unit(k)
        inbox[d, g, row] = turned[d * groups + g, pl.ds(pl.multiple_of(row * a_dev, a_dev), a_dev), :]

        def arrived(p, inner):
            x_copy(d, g, p).wait_recv()
            return inner

        lax.fori_loop(1, n_row, arrived, 0)
        for t in range(tiles):
            parts = [inbox[d, g, t * per_tile + j] for j in range(per_tile)]
            sums = []
            for q in range(per_tile):
                merged = pltpu.roll(parts[0], (-q * a_dev) % LANES, 1) if q else parts[0]
                for j in range(1, per_tile):
                    shift = ((j - q) * a_dev) % LANES
                    moved = pltpu.roll(parts[j], shift, 1) if shift else parts[j]
                    merged = jnp.where(piece == j, moved, merged)
                sums.append(merged)
            here = held(d, g, t)
            here[...] = here[...] + jnp.concatenate(sums, axis=0)

        @pl.when(d > col)
        def _():
            @pl.when(col > 0)
            def _():
                add_from(d, g, True)

            send_on(d, g, True)

        @pl.when(d < col)
        def _():
            @pl.when(col < n_col - 1)
            def _():
                add_from(d, g, False)

            send_on(d, g, False)

        return carry

    lax.fori_loop(0, n_col * groups, combine, 0)

    for g in range(groups):
        @pl.when(col > 0)
        def _(g=g):
            add_from(col, g, True)

        @pl.when(col < n_col - 1)
        def _(g=g):
            add_from(col, g, False)

    for t in range(tiles):
        for a in range(a_dev):
            value = prod[t, pl.ds(col * (share * a_dev) + a, share, stride=a_dev), :]
            at = a * width + t * LANES
            out_ref[:, at:at + LANES] = value.astype(out_ref.dtype)

    def finish(d, carry):
        for g in range(groups):
            def sent(p, inner, g=g):
                x_copy(d, g, p).wait_send()
                return inner

            lax.fori_loop(1, n_row, sent, 0)

            @pl.when(d > col)
            def _(g=g):
                for copy in z_copies(d, g, True):
                    copy.wait_send()

            @pl.when(d < col)
            def _(g=g):
                for copy in z_copies(d, g, False):
                    copy.wait_send()

        return carry

    lax.fori_loop(0, n_col, finish, 0)


def on_device(n_row, n_col, amplitudes, integrals, blocks):
    amplitudes = jnp.swapaxes(amplitudes, 1, 2)
    blocks = blocks.T
    depth, local = integrals.shape
    width = math.isqrt(local * n_row)
    a_dev = width // n_row
    pairs = blocks.shape[1] * OB * OB
    tiles = width // LANES
    share = pairs // n_col
    groups = share * a_dev // LANES
    n_parts = 4
    f32 = jnp.float32
    dma = pltpu.SemaphoreType.DMA
    coded = [
        pltpu.VMEM((n_col, groups, tiles, LANES, LANES), jnp.bfloat16),
        pltpu.VMEM((n_col, groups, tiles // 2, LANES, LANES), jnp.int16),
    ]
    return pl.pallas_call(
        functools.partial(ladder_kernel, n_row, n_col, a_dev),
        out_shape=jax.ShapeDtypeStruct((share, local), jnp.bfloat16),
        in_specs=[
            pl.BlockSpec(memory_space=pltpu.SMEM),
            pl.BlockSpec(memory_space=pl.ANY),
            pl.BlockSpec(memory_space=pl.ANY),
        ],
        out_specs=pl.BlockSpec(memory_space=pltpu.VMEM),
        scratch_shapes=[
            pltpu.VMEM(amplitudes.shape, amplitudes.dtype),
            pltpu.VMEM(integrals.shape, integrals.dtype),
            pltpu.VMEM((2 * pairs, depth), f32),
            pltpu.VMEM((tiles, 2 * pairs * a_dev, LANES), f32),
            pltpu.VMEM((n_col * groups, width, LANES), f32),
            pltpu.VMEM((n_col, groups, n_row, a_dev, LANES), f32),
            *coded, *coded, *coded,
            dma(()),
            dma((n_parts,)),
            dma((n_col, groups, n_row)),
            dma((n_col, groups, n_row)),
            dma((n_col, groups, 2)),
            dma((n_col, groups, 2)),
            dma((n_col, groups, 2)),
            dma((n_col, groups, 2)),
        ],
        compiler_params=pltpu.CompilerParams(
            collective_id=0, has_side_effects=True, vmem_limit_bytes=67043328
        ),
    )(blocks, amplitudes, integrals)


def solution(mesh):
    return jax.shard_map(
        functools.partial(on_device, mesh.shape["row"], mesh.shape["col"]),
        mesh=mesh,
        in_specs=(P(None, None, "col"), P("col", "row"), P()),
        out_specs=P("col", "row"),
        check_vma=False,
    )
```

```python
import functools
import math

import jax
import jax.numpy as jnp
from jax import lax
from jax.experimental import pallas as pl
from jax.experimental.pallas import tpu as pltpu
from jax.sharding import PartitionSpec as P

OB = 2
LANES = 128
CODES = 256.0
SCALE = 256.0 * 127.0
TINY = 1e-30
ROWS = 8


def ladder_kernel(
    n_row, n_col, a_dev,
    blocks, amp_hbm, int_hbm, out_ref,
    amp, ints, lhs, prod, turned, inbox,
    main_out, rest_out, main_left, rest_left, main_right, rest_right,
    amp_sem, int_sem, x_send, x_recv, r_send, r_recv, l_send, l_recv,
):
    row = lax.axis_index("row")
    col = lax.axis_index("col")
    pairs = lhs.shape[0] // 2
    width = a_dev * n_row
    tiles = width // LANES
    per_tile = LANES // a_dev
    share = pairs // n_col
    groups = share // per_tile
    occ = amp.shape[2]
    n_parts = int_sem.shape[0]
    part = ints.shape[1] // n_parts

    barrier = pltpu.get_barrier_semaphore()

    def greet(p, carry):
        pl.semaphore_signal(barrier, inc=1, device_id={"row": lax.rem(row + p, n_row)})
        return carry

    lax.fori_loop(1, n_row, greet, 0)

    @pl.when(col > 0)
    def _():
        pl.semaphore_signal(barrier, inc=1, device_id={"col": col - 1})

    @pl.when(col < n_col - 1)
    def _():
        pl.semaphore_signal(barrier, inc=1, device_id={"col": col + 1})

    amp_copy = pltpu.make_async_copy(amp_hbm, amp, amp_sem)
    amp_copy.start()
    int_copies = []
    for i in range(n_parts):
        cut = pl.ds(i * part, part)
        copy = pltpu.make_async_copy(int_hbm.at[:, cut], ints.at[:, cut], int_sem.at[i])
        if i < n_parts // 2:
            copy.start()
        int_copies.append(copy)

    amp_copy.wait()
    for copy in int_copies[n_parts // 2:]:
        copy.start()
    spot_row = lax.broadcasted_iota(jnp.int32, (ROWS, occ), 0)
    spot_col = lax.broadcasted_iota(jnp.int32, (ROWS, occ), 1)

    def take(spots, plane):
        hit = jnp.zeros((ROWS, occ), jnp.bool_)
        for at, column in spots:
            hit = hit | ((spot_row == at) & (spot_col == column))
        chosen = jnp.where(hit, 1.0, 0.0).astype(amp.dtype)
        return lax.dot_general(
            chosen, amp[plane], (((1,), (1,)), ((), ())), preferred_element_type=jnp.float32
        )

    per_rows = ROWS // (OB * OB)

    def gather(mirrored):
        for tile in range(pairs // ROWS):
            found = jnp.zeros((ROWS, lhs.shape[1]), jnp.float32)
            for k in range(per_rows):
                upper = blocks[0, tile * per_rows + k] * OB
                lower = blocks[1, tile * per_rows + k] * OB
                base = k * OB * OB
                for m in range(OB):
                    if mirrored:
                        found += take([(base + u * OB + m, upper + u) for u in range(OB)], lower + m)
                    else:
                        found += take([(base + m * OB + v, lower + v) for v in range(OB)], upper + m)
            at = (pairs if mirrored else 0) + tile * ROWS
            lhs[at:at + ROWS, :] = found

    gather(True)

    def multiply(i, first):
        block = lhs[first:first + pairs, :].astype(jnp.bfloat16)

        def one(step, carry):
            a = i * (part // width) + step
            panel = ints[:, pl.ds(pl.multiple_of(a * width, width), width)]
            got = jnp.dot(block, panel, preferred_element_type=jnp.float32)
            for t in range(tiles):
                prod[t, pl.ds(first * a_dev + a, pairs, stride=a_dev), :] = got[:, t * LANES:(t + 1) * LANES]
            return carry

        lax.fori_loop(0, part // width, one, 0, unroll=8)

    for i in range(n_parts):
        int_copies[i].wait()
        multiply(i, pairs)

    n_near = jnp.where(col > 0, 1, 0) + jnp.where(col < n_col - 1, 1, 0)
    pl.semaphore_wait(barrier, n_row - 1 + n_near)

    to_right = n_col - 1 - col
    near = jnp.minimum(col, to_right)
    lone = (jnp.maximum(col, to_right) - near) * groups
    outward = jnp.where(to_right >= col, 1, -1)

    def unit(k):
        rest = jnp.maximum(k - lone, 0)
        distance = near - rest // (2 * groups)
        within = rest % (2 * groups)
        side = jnp.where(within % 2 == 0, -outward, outward)
        is_lone = k < lone
        is_own = distance == 0
        shift = jnp.where(is_lone, outward * (near + (lone - 1 - k) // groups + 1), side * distance)
        g = jnp.where(is_lone, k % groups, jnp.where(is_own, within, within // 2))
        return col + shift, g

    def partner(p):
        if n_row & (n_row - 1):
            return lax.rem(row + p, n_row)
        peer, bit = row, 1
        while bit < n_row:
            if p & bit:
                peer = peer + bit - 2 * bit * ((row // bit) % 2)
            bit *= 2
        return peer

    steps = sorted(range(1, n_row), key=lambda p: (-bin(p // 2).count('1'), p))

    def x_copy(d, g, p):
        peer = partner(p)
        return pltpu.make_async_remote_copy(
            src_ref=turned.at[d * groups + g, pl.ds(pl.multiple_of(peer * a_dev, a_dev), a_dev), :],
            dst_ref=inbox.at[d, g, row],
            send_sem=x_send.at[d, g, p],
            recv_sem=x_recv.at[d, g, p],
            device_id={"row": peer},
        )

    def z_copies(d, g, right):
        send, recv = (r_send, r_recv) if right else (l_send, l_recv)
        main_in, rest_in = (main_left, rest_left) if right else (main_right, rest_right)
        to = col + 1 if right else col - 1
        return [
            pltpu.make_async_remote_copy(
                src_ref=src.at[d, g], dst_ref=dst.at[d, g],
                send_sem=send.at[d, g, i], recv_sem=recv.at[d, g, i],
                device_id={"col": to},
            )
            for i, (src, dst) in enumerate(((main_out, main_in), (rest_out, rest_in)))
        ]

    def held(d, g, t):
        start = pl.multiple_of(d * (share * a_dev) + g * LANES, LANES)
        return prod.at[t, pl.ds(start, LANES)]

    half = tiles // 2

    def add_from(d, g, right):
        for copy in z_copies(d, g, right):
            copy.wait_recv()
        main_in, rest_in = (main_left, rest_left) if right else (main_right, rest_right)
        for t in range(half):
            word = rest_in[d, g, t].astype(jnp.int32).astype(jnp.float32)
            high = jnp.round(word * (1.0 / CODES))
            for place, code in ((t, high), (t + half, word - high * CODES)):
                main = main_in[d, g, place].astype(jnp.float32)
                step = jnp.maximum(jnp.abs(main), TINY) * (1.0 / SCALE)
                here = held(d, g, place)
                here[...] = here[...] + (main + code * step)

    def send_on(d, g, right):
        for t in range(half):
            codes = []
            for place in (t, t + half):
                value = held(d, g, place)[...]
                main = value.astype(jnp.bfloat16)
                main_out[d, g, place] = main
                main = main.astype(jnp.float32)
                codes.append(jnp.round((value - main) * (SCALE / jnp.maximum(jnp.abs(main), TINY))))
            word = codes[0] * CODES + codes[1]
            rest_out[d, g, t] = word.astype(jnp.int32).astype(jnp.int16)
        for copy in z_copies(d, g, right):
            copy.start()

    def turn(k, carry):
        d, g = unit(k)
        start = (pairs + d * share + g * per_tile) * a_dev
        for t in range(tiles):
            block = prod[t, pl.ds(pl.multiple_of(start, LANES), LANES), :]
            turned[d * groups + g, t * LANES:(t + 1) * LANES, :] = block.T

        for p in steps:
            x_copy(d, g, p).start()
        return carry

    lax.fori_loop(0, n_col * groups, turn, 0)

    gather(False)
    for i in range(n_parts):
        multiply(i, 0)

    piece = lax.broadcasted_iota(jnp.int32, (a_dev, LANES), 1) // a_dev

    def combine(k, carry):
        d, g = unit(k)
        inbox[d, g, row] = turned[d * groups + g, pl.ds(pl.multiple_of(row * a_dev, a_dev), a_dev), :]

        for p in steps:
            x_copy(d, g, p).wait_recv()
        for t in range(tiles):
            parts = [inbox[d, g, t * per_tile + j] for j in range(per_tile)]
            sums = []
            for q in range(per_tile):
                merged = pltpu.roll(parts[0], (-q * a_dev) % LANES, 1) if q else parts[0]
                for j in range(1, per_tile):
                    shift = ((j - q) * a_dev) % LANES
                    moved = pltpu.roll(parts[j], shift, 1) if shift else parts[j]
                    merged = jnp.where(piece == j, moved, merged)
                sums.append(merged)
            here = held(d, g, t)
            here[...] = here[...] + jnp.concatenate(sums, axis=0)

        @pl.when(d > col)
        def _():
            @pl.when(col > 0)
            def _():
                add_from(d, g, True)

            send_on(d, g, True)

        @pl.when(d < col)
        def _():
            @pl.when(col < n_col - 1)
            def _():
                add_from(d, g, False)

            send_on(d, g, False)

        return carry

    lax.fori_loop(0, n_col * groups, combine, 0)

    for g in range(groups):
        @pl.when(col > 0)
        def _(g=g):
            add_from(col, g, True)

        @pl.when(col < n_col - 1)
        def _(g=g):
            add_from(col, g, False)

    for t in range(tiles):
        for a in range(a_dev):
            value = prod[t, pl.ds(col * (share * a_dev) + a, share, stride=a_dev), :]
            at = a * width + t * LANES
            out_ref[:, at:at + LANES] = value.astype(out_ref.dtype)

    def finish(d, carry):
        for g in range(groups):
            for p in steps:
                x_copy(d, g, p).wait_send()

            @pl.when(d > col)
            def _(g=g):
                for copy in z_copies(d, g, True):
                    copy.wait_send()

            @pl.when(d < col)
            def _(g=g):
                for copy in z_copies(d, g, False):
                    copy.wait_send()

        return carry

    lax.fori_loop(0, n_col, finish, 0)


def on_device(n_row, n_col, amplitudes, integrals, blocks):
    amplitudes = jnp.swapaxes(amplitudes, 1, 2)
    blocks = blocks.T
    depth, local = integrals.shape
    width = math.isqrt(local * n_row)
    a_dev = width // n_row
    pairs = blocks.shape[1] * OB * OB
    tiles = width // LANES
    share = pairs // n_col
    groups = share * a_dev // LANES
    n_parts = 4
    f32 = jnp.float32
    dma = pltpu.SemaphoreType.DMA
    coded = [
        pltpu.VMEM((n_col, groups, tiles, LANES, LANES), jnp.bfloat16),
        pltpu.VMEM((n_col, groups, tiles // 2, LANES, LANES), jnp.int16),
    ]
    return pl.pallas_call(
        functools.partial(ladder_kernel, n_row, n_col, a_dev),
        out_shape=jax.ShapeDtypeStruct((share, local), jnp.bfloat16),
        in_specs=[
            pl.BlockSpec(memory_space=pltpu.SMEM),
            pl.BlockSpec(memory_space=pl.ANY),
            pl.BlockSpec(memory_space=pl.ANY),
        ],
        out_specs=pl.BlockSpec(memory_space=pltpu.VMEM),
        scratch_shapes=[
            pltpu.VMEM(amplitudes.shape, amplitudes.dtype),
            pltpu.VMEM(integrals.shape, integrals.dtype),
            pltpu.VMEM((2 * pairs, depth), f32),
            pltpu.VMEM((tiles, 2 * pairs * a_dev, LANES), f32),
            pltpu.VMEM((n_col * groups, width, LANES), f32),
            pltpu.VMEM((n_col, groups, n_row, a_dev, LANES), f32),
            *coded, *coded, *coded,
            dma(()),
            dma((n_parts,)),
            dma((n_col, groups, n_row)),
            dma((n_col, groups, n_row)),
            dma((n_col, groups, 2)),
            dma((n_col, groups, 2)),
            dma((n_col, groups, 2)),
            dma((n_col, groups, 2)),
        ],
        compiler_params=pltpu.CompilerParams(
            collective_id=0, has_side_effects=True, vmem_limit_bytes=67043328
        ),
    )(blocks, amplitudes, integrals)


def solution(mesh):
    return jax.shard_map(
        functools.partial(on_device, mesh.shape["row"], mesh.shape["col"]),
        mesh=mesh,
        in_specs=(P(None, None, "col"), P("col", "row"), P()),
        out_specs=P("col", "row"),
        check_vma=False,
    )
```
